256 devices in a mesh: sess: 32 (over y_hi, z, core), dp: 4 (over x), fsdp: 2 (over y_lo).
Axes of the slice: x: 4, y: 4 (y_hi: 2, y_lo: 2; y = y_hi * 2 + y_lo), z: 8, core: 2. Of those that a mesh axis runs over, the one named last changes fastest.
Arguments:
- unit_tokens: bfloat16 [4096, 128, 1024], P(('sess', 'dp', 'fsdp')), may hold values from -6 to 6
- block_owner: int32 [4096, 1], P(('sess', 'dp', 'fsdp')), may hold values from 0 to 31; in each aligned block of 16 rows (0 to 15, 16 to 31, ...) at most 2 rows name the same one
- block_clip: int32 [4096], P(('sess', 'dp', 'fsdp')), may hold values from 0 to 1
- block_valid: int32 [4096], P(('sess', 'dp', 'fsdp')), may hold values from 1 to 128, as said below
- latent_query_rows: bfloat16 [32, 1024], replicated, may hold values from -600 to 600
- latents: bfloat16 [32, 1024], replicated, may hold values from -1.5 to 1.5
- w_kv: bfloat16 [1024, 512], P('fsdp'), may hold values from -0.1875 to 0.1875
- w_out: bfloat16 [1024, 1024], P('fsdp'), may hold values from -0.75 to 0.75
- w_proj: bfloat16 [1024, 512], P('fsdp'), may hold values from -0.1875 to 0.1875
- movie_frame_embeddings: bfloat16 [512, 512], replicated, may hold values from -6 to 6
- clip_frame: int32 [512], P(('sess', 'dp', 'fsdp')), may hold values from 0 to 511
- logit_scale: float32 [1], replicated, may hold values from 40 to 60
Outputs:
- latent_state: bfloat16 [512, 32, 1024], P(('sess', 'dp', 'fsdp'))
- clip_loss: float32 [512], P(('sess', 'dp', 'fsdp'))
The draws below stay inside these ranges and needn't reach their ends.
Inputs may be any that keep to these rules, and one draw needn't show every extreme that they name: `block_owner`: among the 16 blocks of one device no index is named more than 2 times, a bound that some block reaches. `block_valid`: the first block of every device is full.
All inputs are finite; a program needn't handle non-finite values.
Results may differ from the reference program's by a relative error of at most 0.009.
The reference program's roundings to bfloat16 on the way count: a program that leaves them out, or rounds other values in their place, can miss the bound.
Values may be sent and summed in bfloat16 or wider, within the bound.
A program may use at most 128 MiB of HBM per device.

```python
import math
import jax
import jax.numpy as jnp
import numpy as np
from jax import lax

D = 1024
HEADS = 16
HEAD_DIM = 64
KV_HEADS = 4
KVW = 256
LAT = 32
ROWS = 128
BLK_DEV = 16
CLIP_DEV = 2
E = 512
FRAMES = 512
CAP = 2
BLOCKS = 4096
CLIPS = 512
N_SESS = 32
N_DP = 4
N_FSDP = 2


def draw_block_valid(key, part):
    first_key, second_key = jax.random.split(key)
    partial_rows = jax.random.randint(first_key, (BLOCKS,), 1, ROWS + 1)
    picker = jax.random.randint(second_key, (BLOCKS,), 0, 3)
    leading = jnp.arange(BLOCKS) % BLK_DEV == 0
    return jnp.where(leading | (picker > 0), ROWS, partial_rows).astype(jnp.int32)


def draw_latent_query_rows(key, part):
    base_key = jax.random.fold_in(key, 0)
    base = jnp.clip(jax.random.normal(base_key, (LAT, D), jnp.float32), -6.0, 6.0)
    return base.astype(jnp.bfloat16)


def touch_ends(drawn, own_key, smallest, largest):
    dims = drawn.shape
    place = [jax.random.randint(jax.random.fold_in(own_key, axis), (), 0, dims[axis]) for axis in range(len(dims))]
    drawn = drawn.at[tuple(place)].set(smallest)
    longest = dims.index(max(dims))
    place[longest] = (place[longest] + 1) % dims[longest]
    return drawn.at[tuple(place)].set(largest)


def block_scale(rng, extent, shards, least, top_value):
    factor_of = 1.0
    for axis_at, shards_of in shards:
        draws = jax.random.uniform(jax.random.fold_in(jax.random.fold_in(rng, 6), axis_at), (shards_of,), jnp.float32, least / len(shards), top_value / len(shards))
        factor_of = factor_of * jnp.repeat(jnp.exp(draws), extent[axis_at] // shards_of).reshape((-1,) + (1,) * (len(extent) - 1 - axis_at))
    return factor_of


def routed_block(own_key, own, number, rows, number_of, top, limit, slope):
    ranking = jax.random.permutation(own_key, number_of)
    crowded, common = load_shares(number_of, rows * top, limit, slope, True), load_shares(number_of, rows * top, limit, slope, False)
    places = jnp.arange(number_of)

    def named(sizes, offset_by):
        used = int((sizes > 0).sum())
        fixed = max(1, used // 4)
        passed = fixed + (places - fixed + offset_by * (used - fixed)) % max(1, number_of - fixed)
        return jnp.zeros((number_of,), jnp.int32).at[ranking[jnp.where(places < fixed, places, passed)]].set(jnp.asarray(sizes, jnp.int32))

    sizes = jnp.where(number % 4 == 0, named(crowded, number // 4), named(common, number - number // 4 - 1))
    mixed = jax.random.permutation(jax.random.fold_in(own, 3), number_of)
    donor, receiver = mixed[0:number_of // 2 * 2:2], mixed[1:number_of // 2 * 2:2]
    margin = jnp.minimum(sizes[donor] - 1, limit - sizes[receiver]) // 2
    margin = jnp.where((donor == ranking[0]) | (receiver == ranking[0]) | (sizes[receiver] == 0), 0, jnp.maximum(margin, 0))
    passed = jax.random.randint(jax.random.fold_in(own, 4), (number_of // 2,), 0, 1 << 20) % (margin + 1)
    sizes = sizes.at[donor].add(-passed).at[receiver].add(passed)
    members = jnp.searchsorted(jnp.cumsum(sizes), jnp.arange(rows * top), side="right").astype(jnp.int32)
    listing = members.reshape(top, rows).T
    listing = listing[jax.random.permutation(jax.random.fold_in(own, 1), rows)]
    offset_by = jax.random.randint(jax.random.fold_in(own, 2), (rows, 1), 0, top)
    return jnp.take_along_axis(listing, (jnp.arange(top)[None, :] + offset_by) % top, axis=1)


def load_shares(amount, total, bound, skew, full):
    portions = [(1 << 20) // math.isqrt(standing ** skew) + 1 for standing in range(1, amount + 1)]
    largest = bound if full else min(bound, max(-(-total // amount), total * portions[0] // sum(portions)))
    least = 1 if total - largest >= amount - 1 else 0
    counts, spare = [largest] + [least] * (amount - 1), total - largest - least * (amount - 1)
    while spare > 0:
        candidates = [i for i in range(1, amount) if counts[i] < largest] or [i for i in range(1, amount) if counts[i] < bound]
        mass, remaining = sum([portions[i] for i in candidates]), spare
        for i in candidates:
            extra = min(bound - counts[i], max(1, remaining * portions[i] // mass), spare)
            counts[i] = counts[i] + extra
            spare = spare - extra
    return np.array(counts)


def scatter_about(key, shape, scale, most, shards=(), held_as=jnp.bfloat16):
    entries = scale * jax.random.normal(key, shape, jnp.float32)
    if shards:
        entries = entries * block_scale(key, shape, shards, -0.22, 0.18)
    return jnp.clip(entries, -most, most).astype(held_as)


def setup_inputs(seed: int = 0) -> dict:
    key_list = jax.random.split(jax.random.key(seed), 13)
    unit_tokens = scatter_about(key_list[0], (BLOCKS, ROWS, D), 1.0, 6.0, ((0, 256),))
    block_owner_keys = jax.random.split(jax.random.fold_in(key_list[1], 1), BLOCKS // BLK_DEV)
    block_owner_turns = jax.random.permutation(jax.random.fold_in(key_list[1], 3), BLOCKS // BLK_DEV)
    block_owner = jax.vmap(lambda own, number: routed_block(jax.random.fold_in(key_list[1], 2), own, number, BLK_DEV, N_SESS, 1, CAP, 2))(block_owner_keys, block_owner_turns).reshape((BLOCKS, 1))
    block_clip = touch_ends(jax.random.randint(key_list[2], (BLOCKS,), 0, CLIP_DEV), jax.random.fold_in(key_list[2], 1), 0, CLIP_DEV - 1).astype(jnp.int32)
    block_valid = draw_block_valid(jax.random.fold_in(key_list[12], 71), 0)
    latent_query_rows = draw_latent_query_rows(jax.random.fold_in(key_list[12], 71), 0)
    latents = scatter_about(key_list[5], (LAT, D), 0.1, 1.5)
    w_kv = scatter_about(key_list[6], (D, 2 * KVW), D ** -0.5, 0.1875, ((0, 2),))
    w_out = scatter_about(key_list[7], (D, D), (D // 16) ** -0.5, 0.75, ((0, 2),))
    w_proj = scatter_about(key_list[8], (D, E), D ** -0.5, 0.1875, ((0, 2),))
    movie_frame_embeddings = scatter_about(key_list[9], (FRAMES, E), 1.0, 6.0)
    clip_frame = touch_ends(jax.random.randint(key_list[10], (CLIPS,), 0, FRAMES), jax.random.fold_in(key_list[10], 1), 0, FRAMES - 1).astype(jnp.int32)
    logit_scale = jnp.clip(jnp.exp(jax.random.uniform(key_list[11], (1,), jnp.float32, math.log(40.0), math.log(60.0))), 40.0, 60.0)
    return {"unit_tokens": unit_tokens, "block_owner": block_owner, "block_clip": block_clip, "block_valid": block_valid, "latent_query_rows": latent_query_rows, "latents": latents, "w_kv": w_kv, "w_out": w_out, "w_proj": w_proj, "movie_frame_embeddings": movie_frame_embeddings, "clip_frame": clip_frame, "logit_scale": logit_scale}


def reference(unit_tokens, block_owner, block_clip, block_valid, latent_query_rows, latents, w_kv, w_out, w_proj, movie_frame_embeddings, clip_frame, logit_scale):
    group_size = HEADS // KV_HEADS
    scaling = 1.0 / math.sqrt(HEAD_DIM)
    kv_all = jnp.dot(unit_tokens.reshape(BLOCKS * ROWS, D), w_kv, preferred_element_type=jnp.float32)
    kv_all = kv_all.astype(jnp.bfloat16).reshape(BLOCKS, ROWS, 2 * KVW)
    spread = N_DP * N_FSDP
    position = jnp.arange(BLOCKS, dtype=jnp.int32)
    owner = block_owner[:, 0] * spread + position // BLK_DEV % spread
    target = (owner * CLIP_DEV + block_clip).astype(jnp.int32)
    query = latent_query_rows.astype(jnp.float32).reshape(LAT, KV_HEADS, group_size, HEAD_DIM)
    row_index = jnp.arange(ROWS, dtype=jnp.int32)

    def scores_of(kv_block, valid):
        keys = kv_block[:, :KVW].astype(jnp.float32).reshape(ROWS, KV_HEADS, HEAD_DIM)
        scores = jnp.einsum('lkjd,rkd->kjlr', query, keys) * scaling
        return jnp.where((row_index < valid)[None, None, None, :], scores, -jnp.inf)

    def first_pass(top, item):
        kv_block, valid, clip_id = item
        scores = scores_of(kv_block, valid)
        return (top.at[clip_id].max(lax.optimization_barrier(jnp.max(scores, axis=-1))), None)
    top_init = jnp.zeros((CLIPS, KV_HEADS, group_size, LAT), jnp.float32)
    top, _ = lax.scan(first_pass, top_init, (kv_all, block_valid, target))

    def second_pass(carry, item):
        numer, denom = carry
        kv_block, valid, clip_id = item
        scores = scores_of(kv_block, valid)
        terms = jnp.exp(scores - top[clip_id][..., None])
        value_rows = kv_block[:, KVW:].astype(jnp.float32).reshape(ROWS, KV_HEADS, HEAD_DIM)
        rounded_result = lax.optimization_barrier(terms.astype(jnp.bfloat16)).astype(jnp.float32)
        part = jnp.einsum('kjlr,rkd->kjld', rounded_result, value_rows)
        return ((numer.at[clip_id].add(part), denom.at[clip_id].add(lax.optimization_barrier(jnp.sum(terms, axis=-1)))), None)
    numer_init = jnp.zeros((CLIPS, KV_HEADS, group_size, LAT, HEAD_DIM), jnp.float32)
    denom_init = jnp.zeros((CLIPS, KV_HEADS, group_size, LAT), jnp.float32)
    (numer, denom), _ = lax.scan(second_pass, (numer_init, denom_init), (kv_all, block_valid, target))
    totals = denom + jnp.exp(-top)
    attention = numer / totals[..., None]
    attention = jnp.transpose(attention, (0, 3, 1, 2, 4)).reshape(CLIPS, LAT, D).astype(jnp.bfloat16)
    mixed = jnp.dot(attention.reshape(CLIPS * LAT, D), w_out, preferred_element_type=jnp.float32)
    state = latents.astype(jnp.float32)[None] + mixed.reshape(CLIPS, LAT, D)
    latent_state = state.astype(jnp.bfloat16)
    pooled = lax.optimization_barrier(jnp.mean(state, axis=1)).astype(jnp.bfloat16)
    embed = jnp.dot(pooled, w_proj, preferred_element_type=jnp.float32)
    embed_unit = (embed / jnp.sqrt(lax.optimization_barrier(jnp.sum(embed * embed, axis=-1, keepdims=True)) + 1e-06)).astype(jnp.bfloat16)
    frames = movie_frame_embeddings[clip_frame].astype(jnp.float32)
    frame_unit = (frames / jnp.sqrt(lax.optimization_barrier(jnp.sum(frames * frames, axis=-1, keepdims=True)) + 1e-06)).astype(jnp.bfloat16)
    logits = logit_scale[0] * jnp.dot(embed_unit, frame_unit.T, preferred_element_type=jnp.float32)
    row_lse = jax.nn.logsumexp(logits, axis=1)
    col_lse = jax.nn.logsumexp(logits, axis=0)
    clip_loss = 0.5 * (row_lse + col_lse) - jnp.diagonal(logits)
    return (latent_state, clip_loss)
```

```python
import jax
import jax.numpy as jnp
from jax import lax
from jax.experimental import pallas as pl
from jax.experimental.pallas import tpu as pltpu
from jax.sharding import PartitionSpec as P

HEADS = 16
HEAD_DIM = 64
KV_HEADS = 4
GROUP = HEADS // KV_HEADS
NZ = 8
NY = 2
NC = 2
PEERS = NY * NZ * NC
F32 = jnp.float32
BF16 = jnp.bfloat16
MESH = pl.DeviceIdType.MESH
VMEM_SPEC = pl.BlockSpec(memory_space=pltpu.VMEM)
SMEM_SPEC = pl.BlockSpec(memory_space=pltpu.SMEM)


def place():
    sess = lax.axis_index("sess")
    y_hi = sess // (NZ * NC)
    z = (sess // NC) % NZ
    core = sess % NC
    return sess, y_hi, z, core


def sess_of(y_hi, z, core):
    return (y_hi * NZ + z) * NC + core


def remote(src, dst, send_sem, recv_sem, where):
    return pltpu.make_async_remote_copy(
        src_ref=src, dst_ref=dst, send_sem=send_sem, recv_sem=recv_sem, device_id=where, device_id_type=MESH
    )


def weight_peers():
    sess, y_hi, z, core = place()
    half = lax.axis_index("fsdp")
    near = {"sess": sess, "fsdp": 1 - half}
    far = {"sess": sess_of(1 - y_hi, z, core), "fsdp": 1 - half}
    twin = {"sess": sess_of(y_hi, z, 1 - core)}
    return half, core, near, far, twin


def weight_copies(src, out, send, recv):
    half, core, near, far, twin = weight_peers()
    first = [
        remote(src.at[2 * core + i], out.at[half, 2 * core + i], send.at[i], recv.at[i], to)
        for i, to in enumerate((near, far))
    ]
    relay = [
        remote(
            out.at[1 - half, 2 * core + i], out.at[1 - half, 2 * core + i], send.at[2 + i], recv.at[2 + i], twin
        )
        for i in range(2)
    ]
    return first, relay


def kv_weight_kernel(w_ref, out_ref, send, recv, local):
    half, core, near, far, twin = weight_peers()
    barrier = pltpu.get_barrier_semaphore()
    for to in (near, far, twin):
        pl.semaphore_signal(barrier, inc=1, device_id=to, device_id_type=MESH)
    own = pltpu.make_async_copy(w_ref, out_ref.at[half], local)
    own.start()
    pl.semaphore_wait(barrier, 3)
    first, relay = weight_copies(w_ref, out_ref, send, recv)
    for c in first:
        c.start()
    for c, r in zip(first, relay):
        c.wait_recv()
        r.start()
    for r in relay:
        r.wait_recv()
    for c in first + relay:
        c.wait_send()
    own.wait()


def gather_kv_weight(w):
    rows, cols = w.shape
    quarter = rows // 4
    out = pl.pallas_call(
        kv_weight_kernel,
        name="kv_weight",
        out_shape=jax.ShapeDtypeStruct((2, 4, quarter, cols), w.dtype),
        in_specs=[VMEM_SPEC],
        out_specs=VMEM_SPEC,
        scratch_shapes=[
            pltpu.SemaphoreType.DMA((4,)),
            pltpu.SemaphoreType.DMA((4,)),
            pltpu.SemaphoreType.DMA,
        ],
        compiler_params=pltpu.CompilerParams(collective_id=0, has_side_effects=True),
    )(w.reshape(4, quarter, cols))
    return out.reshape(2 * rows, cols)


def project_kernel(per, owner, clip, valid, x_ref, w_ref, q_ref, kv_ref, tops_ref, qt_ref):
    step = pl.program_id(0)
    rows = x_ref.shape[1]
    lat = q_ref.shape[0]

    @pl.when(step == 0)
    def _():
        tops_ref[...] = jnp.zeros_like(tops_ref)
        qt_ref[...] = jnp.zeros_like(qt_ref)
        qt = (q_ref[...].astype(F32) * (HEAD_DIM**-0.5)).T.astype(BF16)
        for head in range(HEADS):
            kh, j = head // GROUP, head % GROUP
            pair, inner = kh // 2, kh % 2
            qt_ref[
                pair,
                inner * HEAD_DIM : (inner + 1) * HEAD_DIM,
                inner * GROUP * lat + j * lat : inner * GROUP * lat + (j + 1) * lat,
            ] = qt[head * HEAD_DIM : (head + 1) * HEAD_DIM, :]

    kv = jnp.dot(x_ref[...].reshape(per * rows, x_ref.shape[2]), w_ref[...], preferred_element_type=F32)
    kv = kv.astype(BF16)
    kv_ref[...] = kv.reshape(per, rows, kv.shape[1])
    row = lax.broadcasted_iota(jnp.int32, (rows, 1), 0)
    for pair in range(2):
        scores = jnp.dot(kv[:, pair * 128 : (pair + 1) * 128], qt_ref[pair], preferred_element_type=F32)
        for i in range(per):
            block = step * per + i
            slot = owner[block] * 2 + clip[block]
            part = scores[i * rows : (i + 1) * rows, :]
            top = jnp.max(jnp.where(row < valid[block], part, 0.0), axis=0, keepdims=True)
            for inner in range(2):
                kh = pair * 2 + inner
                now = tops_ref[slot, kh : kh + 1, :]
                tops_ref[slot, kh : kh + 1, :] = jnp.maximum(now, top[:, inner * 128 : (inner + 1) * 128])


def project(owner, clip, valid, x, w, q):
    blocks, rows, width = x.shape
    cols = w.shape[1]
    per = 2
    return pl.pallas_call(
        lambda *refs: project_kernel(per, *refs),
        name="project",
        grid_spec=pltpu.PrefetchScalarGridSpec(
            num_scalar_prefetch=3,
            grid=(blocks // per,),
            in_specs=[
                pl.BlockSpec((per, rows, width), lambda i, *_: (i, 0, 0)),
                pl.BlockSpec((width, cols), lambda i, *_: (0, 0)),
                pl.BlockSpec(q.shape, lambda i, *_: (0, 0)),
            ],
            out_specs=[
                pl.BlockSpec((per, rows, cols), lambda i, *_: (i, 0, 0)),
                pl.BlockSpec((PEERS * 2, 4, 128), lambda i, *_: (0, 0, 0)),
                pl.BlockSpec((2, 128, 256), lambda i, *_: (0, 0, 0)),
            ],
        ),
        out_shape=[
            jax.ShapeDtypeStruct((blocks, rows, cols), BF16),
            jax.ShapeDtypeStruct((PEERS * 2, 4, 128), F32),
            jax.ShapeDtypeStruct((2, 128, 256), BF16),
        ],
    )(owner, clip, valid, x, w, q)


def tops_kernel(mine_ref, all_ref, own_ref, inbox, send, recv, send2, recv2):
    sess, *_ = place()
    barrier = pltpu.get_barrier_semaphore()

    def signal(k, _):
        pl.semaphore_signal(
            barrier, inc=1, device_id={"sess": lax.rem(sess + k, PEERS)}, device_id_type=MESH
        )
        return _

    lax.fori_loop(1, PEERS, signal, 0)
    pl.semaphore_wait(barrier, PEERS - 1)

    def copy_in(k):
        to = lax.rem(sess + k, PEERS)
        return remote(mine_ref.at[to], inbox.at[k], send.at[k], recv.at[k], {"sess": to})

    def copy_out(k):
        to = lax.rem(sess + k, PEERS)
        return remote(own_ref, all_ref.at[sess], send2.at[k], recv2.at[k], {"sess": to})

    def arrival(k):
        source = lax.rem(sess + PEERS - k, PEERS)
        return remote(own_ref, all_ref.at[source], send2.at[k], recv2.at[k], {"sess": source})

    def start(k, _):
        copy_in(k).start()
        return _

    lax.fori_loop(1, PEERS, start, 0)

    def gather(k, top):
        copy_in(k).wait_recv()
        return jnp.maximum(top, inbox[k])

    top = lax.fori_loop(1, PEERS, gather, mine_ref[sess])
    own_ref[...] = top

    def start2(k, _):
        copy_out(k).start()
        return _

    lax.fori_loop(1, PEERS, start2, 0)
    all_ref[sess] = top

    def finish(k, _):
        copy_in(k).wait_send()
        copy_out(k).wait_send()
        arrival(k).wait_recv()
        return _

    lax.fori_loop(1, PEERS, finish, 0)


def exchange_tops(tops):
    return pl.pallas_call(
        tops_kernel,
        name="tops",
        out_shape=[
            jax.ShapeDtypeStruct((PEERS, 2, 4, 128), F32),
            jax.ShapeDtypeStruct((2, 4, 128), F32),
        ],
        in_specs=[VMEM_SPEC],
        out_specs=[VMEM_SPEC, VMEM_SPEC],
        scratch_shapes=[pltpu.VMEM((PEERS, 2, 4, 128), F32)] + [pltpu.SemaphoreType.DMA((PEERS,))] * 4,
        compiler_params=pltpu.CompilerParams(collective_id=1, has_side_effects=True),
    )(tops.reshape(PEERS, 2, 4, 128))


SUB = 264


def weigh_kernel(per, owner, clip, valid, kv_ref, tops_ref, qt_ref, out_ref):
    step = pl.program_id(0)
    rows = kv_ref.shape[1]

    @pl.when(step == 0)
    def _():
        out_ref[...] = jnp.zeros_like(out_ref)

    row = lax.broadcasted_iota(jnp.int32, (rows, 1), 0)
    for i in range(per):
        block = step * per + i
        who = owner[block]
        y_hi, z, core = who // (NZ * NC), (who // NC) % NZ, who % NC
        slot = ((core * NZ + z) * NY + y_hi) * 2 + clip[block]
        live = row < valid[block]
        for pair in range(2):
            scores = jnp.dot(
                kv_ref[i, :, pair * 128 : (pair + 1) * 128], qt_ref[pair], preferred_element_type=F32
            )
            values = kv_ref[i, :, 256 + pair * 128 : 256 + (pair + 1) * 128].astype(F32).T.astype(BF16)
            for inner in range(2):
                kh = pair * 2 + inner
                top = tops_ref[who * 2 + clip[block], kh : kh + 1, :]
                prob = jnp.where(live, jnp.exp(scores[:, inner * 128 : (inner + 1) * 128] - top), 0.0)
                total = jnp.sum(prob, axis=0, keepdims=True)
                part = jnp.dot(
                    values[inner * HEAD_DIM : (inner + 1) * HEAD_DIM, :],
                    prob.astype(BF16),
                    preferred_element_type=F32,
                )
                out_ref[slot, kh * HEAD_DIM : (kh + 1) * HEAD_DIM, :] += part
                out_ref[slot, 256 + kh : 257 + kh, :] += total


def weigh(owner, clip, valid, kv, tops, qt):
    blocks, rows, cols = kv.shape
    per = 2
    return pl.pallas_call(
        lambda *refs: weigh_kernel(per, *refs),
        name="weigh",
        grid_spec=pltpu.PrefetchScalarGridSpec(
            num_scalar_prefetch=3,
            grid=(blocks // per,),
            in_specs=[
                pl.BlockSpec((per, rows, cols), lambda i, *_: (i, 0, 0)),
                pl.BlockSpec((PEERS * 2, 4, 128), lambda i, *_: (0, 0, 0)),
                pl.BlockSpec((2, 128, 256), lambda i, *_: (0, 0, 0)),
            ],
            out_specs=pl.BlockSpec((PEERS * 2, SUB, 128), lambda i, *_: (0, 0, 0)),
        ),
        out_shape=jax.ShapeDtypeStruct((PEERS * 2, SUB, 128), F32),
    )(owner, clip, valid, kv, tops, qt)


ORDER = (4, 3, 5, 2, 6, 1, 7, 0)


def reduce_kernel(
    part_ref, wo_ref, wp_ref, out_ref, wo_out, wp_out,
    twin_in, run, chain_in, y_in, final,
    csend, crecv, zsend, zrecv, ysend, yrecv, wsend, wrecv, local,
):
    sess, y_hi, z, core = place()
    half, _, near, far, twin = weight_peers()
    up = {"sess": sess_of(y_hi, lax.rem(z + 1, NZ), core)}
    down = {"sess": sess_of(y_hi, lax.rem(z + NZ - 1, NZ), core)}
    across = {"sess": sess_of(1 - y_hi, z, core)}
    barrier = pltpu.get_barrier_semaphore()
    for to in (near, far, twin, up, down, across):
        pl.semaphore_signal(barrier, inc=1, device_id=to, device_id_type=MESH)
    owns = [
        pltpu.make_async_copy(wo_ref, wo_out.at[half], local.at[0]),
        pltpu.make_async_copy(wp_ref, wp_out.at[half], local.at[1]),
    ]
    for c in owns:
        c.start()
    pl.semaphore_wait(barrier, 6)

    to_twin = {}
    for k in ORDER:
        dest = lax.rem(z + k, NZ)
        to_twin[k] = remote(part_ref.at[1 - core, dest], twin_in.at[k], csend.at[k], crecv.at[k], twin)
        to_twin[k].start()
    weights = []
    for i, (src, out) in enumerate(((wo_ref, wo_out), (wp_ref, wp_out))):
        weights.append(weight_copies(src, out, wsend.at[i], wrecv.at[i]))
        for c in weights[i][0]:
            c.start()

    sent = {}
    ways = (up, down)

    def own_sum(k, sub):
        return part_ref[core, lax.rem(z + k, NZ), sub] + twin_in[k, sub]

    def pass_on(way, hop, sub, value):
        run[way, hop, sub] = value
        c = remote(
            run.at[way, hop, sub],
            chain_in.at[way, hop, sub],
            zsend.at[way, hop, sub],
            zrecv.at[way, hop, sub],
            ways[way],
        )
        c.start()
        sent[way, hop, sub] = c

    to_twin[4].wait_recv()
    for sub in range(2):
        pass_on(0, 0, sub, own_sum(4, sub))
        pass_on(1, 0, 2 + sub, own_sum(4, 2 + sub))
    for hop in range(1, 4):
        ks = (4 - hop, NZ - (4 - hop))
        for k in ks:
            to_twin[k].wait_recv()
        for turn in range(4):
            for way in range(2):
                sub = (turn + 2) % 4 if way == 0 else turn
                value = own_sum(ks[way], sub)
                if (way, hop - 1, sub) in sent:
                    sent[way, hop - 1, sub].wait_recv()
                    value = value + chain_in[way, hop - 1, sub]
                pass_on(way, hop, sub, value)
        if hop == 1:
            for first, relay in weights:
                for c, r in zip(first, relay):
                    c.wait_recv()
                    r.start()

    to_twin[0].wait_recv()
    for sub in range(4):
        value = own_sum(0, sub)
        for way in range(2):
            sent[way, 3, sub].wait_recv()
            value = value + chain_in[way, 3, sub]
        final[sub] = value
    over = []
    for i in range(2):
        c = remote(final.at[(1 - y_hi) * 2 + i], y_in.at[i], ysend.at[i], yrecv.at[i], across)
        c.start()
        over.append(c)
    for i in range(2):
        over[i].wait_recv()
        out_ref[i] = final[y_hi * 2 + i] + y_in[i]

    for c in over:
        c.wait_send()
    for c in sent.values():
        c.wait_send()
    for c in to_twin.values():
        c.wait_send()
    for first, relay in weights:
        for r in relay:
            r.wait_recv()
        for c in first + relay:
            c.wait_send()
    for c in owns:
        c.wait()


def reduce_to_owner(parts, w_out, w_proj):
    wo = w_out.reshape(4, w_out.shape[0] // 4, w_out.shape[1])
    wp = w_proj.reshape(4, w_proj.shape[0] // 4, w_proj.shape[1])
    dma = pltpu.SemaphoreType.DMA
    sums, wo_all, wp_all = pl.pallas_call(
        reduce_kernel,
        name="reduce",
        out_shape=[
            jax.ShapeDtypeStruct((2, SUB, 128), F32),
            jax.ShapeDtypeStruct((2,) + wo.shape, wo.dtype),
            jax.ShapeDtypeStruct((2,) + wp.shape, wp.dtype),
        ],
        in_specs=[VMEM_SPEC] * 3,
        out_specs=[VMEM_SPEC] * 3,
        scratch_shapes=[
            pltpu.VMEM((NZ, 4, SUB, 128), F32),
            pltpu.VMEM((2, 4, 4, SUB, 128), F32),
            pltpu.VMEM((2, 4, 4, SUB, 128), F32),
            pltpu.VMEM((2, SUB, 128), F32),
            pltpu.VMEM((4, SUB, 128), F32),
            dma((NZ,)),
            dma((NZ,)),
            dma((2, 4, 4)),
            dma((2, 4, 4)),
            dma((2,)),
            dma((2,)),
            dma((2, 4)),
            dma((2, 4)),
            dma((2,)),
        ],
        compiler_params=pltpu.CompilerParams(collective_id=2, has_side_effects=True),
    )(parts.reshape(NC, NZ, NY * 2, SUB, 128), wo, wp)
    return sums, wo_all.reshape(-1, w_out.shape[1]), wp_all.reshape(-1, w_proj.shape[1])


def embed_kernel(
    frame, scale, sums_ref, top_ref, lat_ref, wo_ref, wp_ref, movie_ref, state_ref, msg_ref, logit_ref, pick_ref, attn
):
    lat = lat_ref.shape[0]
    for c in range(2):
        columns = []
        for kh in range(KV_HEADS):
            total = sums_ref[c, 256 + kh : 257 + kh, :] + jnp.exp(-top_ref[c, kh : kh + 1, :])
            columns.append(sums_ref[c, kh * HEAD_DIM : (kh + 1) * HEAD_DIM, :] / total)
        turned = jnp.concatenate(columns, axis=0).T.astype(BF16)
        for head in range(HEADS):
            kh, j = head // GROUP, head % GROUP
            attn[c * lat : (c + 1) * lat, head * HEAD_DIM : (head + 1) * HEAD_DIM] = turned[
                j * lat : (j + 1) * lat, kh * HEAD_DIM : (kh + 1) * HEAD_DIM
            ]
    mixed = jnp.dot(attn[...], wo_ref[...], preferred_element_type=F32)
    row = lax.broadcasted_iota(jnp.int32, (16, 1), 0)
    pooled = jnp.zeros((16, mixed.shape[1]), F32)
    for c in range(2):
        state = lat_ref[...].astype(F32) + mixed[c * lat : (c + 1) * lat]
        state_ref[c] = state.astype(BF16)
        pooled = jnp.where(row == c, jnp.mean(state, axis=0, keepdims=True), pooled)
    z = jnp.dot(pooled.astype(BF16), wp_ref[...], preferred_element_type=F32)
    zn = (z / jnp.sqrt(jnp.sum(z * z, axis=-1, keepdims=True) + 1e-06)).astype(BF16)
    movie = movie_ref[...].astype(F32)
    tn = (movie / jnp.sqrt(jnp.sum(movie * movie, axis=-1, keepdims=True) + 1e-06)).astype(BF16)
    logits = lax.dot_general(zn, tn, (((1,), (1,)), ((), ())), preferred_element_type=F32) * scale[0]
    lane = lax.broadcasted_iota(jnp.int32, (1, 128), 1)
    for r in range(4):
        piece = logits[:, r * 128 : (r + 1) * 128]
        msg_ref[r : r + 1, :] = jnp.exp(piece[0:1]) + jnp.exp(piece[1:2])
        picks = []
        for c in range(2):
            picks.append((lane + r * 128 == frame[c]).astype(F32))
            logit_ref[c * 4 + r : c * 4 + r + 1, :] = piece[c : c + 1]
            pick_ref[c * 4 + r : c * 4 + r + 1, :] = picks[c]
        msg_ref[4 + r : 5 + r, :] = picks[0] + picks[1]


def embed(frame, scale, sums, top, latents, w_out, w_proj, movie):
    lat, width = latents.shape
    small = jax.ShapeDtypeStruct((8, 128), F32)
    return pl.pallas_call(
        embed_kernel,
        name="embed",
        out_shape=[jax.ShapeDtypeStruct((2, lat, width), BF16), small, small, small],
        in_specs=[SMEM_SPEC, SMEM_SPEC] + [VMEM_SPEC] * 6,
        out_specs=[VMEM_SPEC] * 4,
        scratch_shapes=[pltpu.VMEM((2 * lat, width), BF16)],
    )(frame, scale, sums, top, latents, w_out, w_proj, movie)


def loss_kernel(msg_ref, logit_ref, pick_ref, out_ref, inbox, inbox2, column, send, recv, send2, recv2):
    sess, y_hi, z, core = place()
    x, half = lax.axis_index("dp"), lax.axis_index("fsdp")
    spots = NY * NC * 4 * 2
    here = ((y_hi * NC + core) * 4 + x) * 2 + half

    def along(k):
        return {"sess": sess_of(y_hi, lax.rem(z + k, NZ), core)}

    def plane(k):
        at = lax.rem(here + k, spots)
        return {
            "sess": sess_of(at // (NC * 8), z, (at // 8) % NC),
            "dp": (at // 2) % 4,
            "fsdp": at % 2,
        }

    barrier = pltpu.get_barrier_semaphore()

    def signal_z(k, _):
        pl.semaphore_signal(barrier, inc=1, device_id=along(k), device_id_type=MESH)
        return _

    def signal_p(k, _):
        pl.semaphore_signal(barrier, inc=1, device_id=plane(k), device_id_type=MESH)
        return _

    lax.fori_loop(1, NZ, signal_z, 0)
    lax.fori_loop(1, spots, signal_p, 0)
    pl.semaphore_wait(barrier, NZ - 1 + spots - 1)

    def copy_z(k):
        return remote(msg_ref, inbox.at[k], send.at[k], recv.at[k], along(k))

    def copy_p(k):
        return remote(column, inbox2.at[k], send2.at[k], recv2.at[k], plane(k))

    def start_z(k, _):
        copy_z(k).start()
        return _

    def add_z(k, total):
        copy_z(k).wait_recv()
        return total + inbox[k]

    def start_p(k, _):
        copy_p(k).start()
        return _

    def add_p(k, total):
        copy_p(k).wait_recv()
        return total + inbox2[k]

    lax.fori_loop(1, NZ, start_z, 0)
    total = lax.fori_loop(1, NZ, add_z, msg_ref[...])
    column[...] = total
    lax.fori_loop(1, spots, start_p, 0)
    total = lax.fori_loop(1, spots, add_p, total)

    def whole(v):
        return jnp.sum(jnp.sum(v, axis=1, keepdims=True), axis=0, keepdims=True)

    for c in range(2):
        logit, pick = logit_ref[c * 4 : c * 4 + 4, :], pick_ref[c * 4 : c * 4 + 4, :]
        row_sum = whole(total[4:8] * jnp.exp(logit))
        col_sum = whole(total[0:4] * pick)
        loss = 0.5 * (jnp.log(row_sum) + jnp.log(col_sum)) - whole(logit * pick)
        out_ref[c : c + 1, :] = jnp.broadcast_to(loss, (1, 128))

    def end_z(k, _):
        copy_z(k).wait_send()
        return _

    def end_p(k, _):
        copy_p(k).wait_send()
        return _

    lax.fori_loop(1, NZ, end_z, 0)
    lax.fori_loop(1, spots, end_p, 0)


def clip_losses(msg, logits, picks):
    dma = pltpu.SemaphoreType.DMA
    spots = NY * NC * 8
    return pl.pallas_call(
        loss_kernel,
        name="loss",
        out_shape=jax.ShapeDtypeStruct((2, 128), F32),
        in_specs=[VMEM_SPEC] * 3,
        out_specs=VMEM_SPEC,
        scratch_shapes=[
            pltpu.VMEM((NZ, 8, 128), F32),
            pltpu.VMEM((spots, 8, 128), F32),
            pltpu.VMEM((8, 128), F32),
            dma((NZ,)),
            dma((NZ,)),
            dma((spots,)),
            dma((spots,)),
        ],
        compiler_params=pltpu.CompilerParams(collective_id=3, has_side_effects=True),
    )(msg, logits, picks)


def per_device(
    unit_tokens,
    block_owner,
    block_clip,
    block_valid,
    latent_query_rows,
    latents,
    w_kv,
    w_out,
    w_proj,
    movie_frame_embeddings,
    clip_frame,
    logit_scale,
):
    owner = block_owner.reshape(-1)
    weight = gather_kv_weight(w_kv)
    kv, tops, qt = project(owner, block_clip, block_valid, unit_tokens, weight, latent_query_rows)
    all_tops, own_top = exchange_tops(tops)
    parts = weigh(owner, block_clip, block_valid, kv, all_tops.reshape(PEERS * 2, 4, 128), qt)
    sums, wo, wp = reduce_to_owner(parts, w_out, w_proj)
    state, msg, logits, picks = embed(
        clip_frame, logit_scale, sums, own_top, latents, wo, wp, movie_frame_embeddings
    )
    loss = clip_losses(msg, logits, picks)
    return state, loss[:, 0]


def solution(mesh):
    return jax.shard_map(
        per_device,
        mesh=mesh,
        in_specs=(
            P(("sess", "dp", "fsdp"), None, None),
            P(("sess", "dp", "fsdp"), None),
            P(("sess", "dp", "fsdp")),
            P(("sess", "dp", "fsdp")),
            P(),
            P(),
            P("fsdp", None),
            P("fsdp", None),
            P("fsdp", None),
            P(),
            P(("sess", "dp", "fsdp")),
            P(),
        ),
        out_specs=(P(("sess", "dp", "fsdp"), None, None), P(("sess", "dp", "fsdp"))),
        check_vma=False,
    )
```

```python
import jax
import jax.numpy as jnp
from jax import lax
from jax.experimental import pallas as pl
from jax.experimental.pallas import tpu as pltpu
from jax.sharding import PartitionSpec as P

HEADS = 16
HEAD_DIM = 64
KV_HEADS = 4
GROUP = HEADS // KV_HEADS
NZ = 8
NY = 2
NC = 2
PEERS = NY * NZ * NC
F32 = jnp.float32
BF16 = jnp.bfloat16
MESH = pl.DeviceIdType.MESH
VMEM_SPEC = pl.BlockSpec(memory_space=pltpu.VMEM)
SMEM_SPEC = pl.BlockSpec(memory_space=pltpu.SMEM)


def place():
    sess = lax.axis_index("sess")
    y_hi = sess // (NZ * NC)
    z = (sess // NC) % NZ
    core = sess % NC
    return sess, y_hi, z, core


def sess_of(y_hi, z, core):
    return (y_hi * NZ + z) * NC + core


def remote(src, dst, send_sem, recv_sem, where):
    return pltpu.make_async_remote_copy(
        src_ref=src, dst_ref=dst, send_sem=send_sem, recv_sem=recv_sem, device_id=where, device_id_type=MESH
    )


def weight_peers():
    sess, y_hi, z, core = place()
    half = lax.axis_index("fsdp")
    near = {"sess": sess, "fsdp": 1 - half}
    far = {"sess": sess_of(1 - y_hi, z, core), "fsdp": 1 - half}
    twin = {"sess": sess_of(y_hi, z, 1 - core)}
    return half, core, near, far, twin


def weight_copies(src, out, send, recv):
    half, core, near, far, twin = weight_peers()
    first = [
        remote(src.at[2 * core + i], out.at[half, 2 * core + i], send.at[i], recv.at[i], to)
        for i, to in enumerate((near, far))
    ]
    relay = [
        remote(
            out.at[1 - half, 2 * core + i], out.at[1 - half, 2 * core + i], send.at[2 + i], recv.at[2 + i], twin
        )
        for i in range(2)
    ]
    return first, relay


def kv_weight_kernel(w_ref, out_ref, send, recv, local):
    half, core, near, far, twin = weight_peers()
    barrier = pltpu.get_barrier_semaphore()
    for to in (near, far, twin):
        pl.semaphore_signal(barrier, inc=1, device_id=to, device_id_type=MESH)
    own = pltpu.make_async_copy(w_ref, out_ref.at[half], local)
    own.start()
    pl.semaphore_wait(barrier, 3)
    first, relay = weight_copies(w_ref, out_ref, send, recv)
    for c in first:
        c.start()
    for c, r in zip(first, relay):
        c.wait_recv()
        r.start()
    for r in relay:
        r.wait_recv()
    for c in first + relay:
        c.wait_send()
    own.wait()


def gather_kv_weight(w):
    rows, cols = w.shape
    quarter = rows // 4
    out = pl.pallas_call(
        kv_weight_kernel,
        name="kv_weight",
        out_shape=jax.ShapeDtypeStruct((2, 4, quarter, cols), w.dtype),
        in_specs=[VMEM_SPEC],
        out_specs=VMEM_SPEC,
        scratch_shapes=[
            pltpu.SemaphoreType.DMA((4,)),
            pltpu.SemaphoreType.DMA((4,)),
            pltpu.SemaphoreType.DMA,
        ],
        compiler_params=pltpu.CompilerParams(collective_id=0, has_side_effects=True),
    )(w.reshape(4, quarter, cols))
    return out.reshape(2 * rows, cols)


def project_kernel(per, owner, clip, valid, x_ref, w_ref, q_ref, kv_ref, tops_ref, qt_ref):
    step = pl.program_id(0)
    rows = x_ref.shape[1]
    lat = q_ref.shape[0]

    @pl.when(step == 0)
    def _():
        tops_ref[...] = jnp.zeros_like(tops_ref)
        qt_ref[...] = jnp.zeros_like(qt_ref)
        qt = (q_ref[...].astype(F32) * (HEAD_DIM**-0.5)).T.astype(BF16)
        for head in range(HEADS):
            kh, j = head // GROUP, head % GROUP
            pair, inner = kh // 2, kh % 2
            qt_ref[
                pair,
                inner * HEAD_DIM : (inner + 1) * HEAD_DIM,
                inner * GROUP * lat + j * lat : inner * GROUP * lat + (j + 1) * lat,
            ] = qt[head * HEAD_DIM : (head + 1) * HEAD_DIM, :]

    kv = jnp.dot(x_ref[...].reshape(per * rows, x_ref.shape[2]), w_ref[...], preferred_element_type=F32)
    kv = kv.astype(BF16)
    kv_ref[...] = kv.reshape(per, rows, kv.shape[1])
    row = lax.broadcasted_iota(jnp.int32, (rows, 1), 0)
    for pair in range(2):
        scores = jnp.dot(kv[:, pair * 128 : (pair + 1) * 128], qt_ref[pair], preferred_element_type=F32)
        for i in range(per):
            block = step * per + i
            slot = owner[block] * 2 + clip[block]
            part = scores[i * rows : (i + 1) * rows, :]
            top = jnp.max(jnp.where(row < valid[block], part, 0.0), axis=0, keepdims=True)
            for inner in range(2):
                kh = pair * 2 + inner
                now = tops_ref[slot, kh : kh + 1, :]
                tops_ref[slot, kh : kh + 1, :] = jnp.maximum(now, top[:, inner * 128 : (inner + 1) * 128])


def project(owner, clip, valid, x, w, q):
    blocks, rows, width = x.shape
    cols = w.shape[1]
    per = 2
    return pl.pallas_call(
        lambda *refs: project_kernel(per, *refs),
        name="project",
        grid_spec=pltpu.PrefetchScalarGridSpec(
            num_scalar_prefetch=3,
            grid=(blocks // per,),
            in_specs=[
                pl.BlockSpec((per, rows, width), lambda i, *_: (i, 0, 0)),
                pl.BlockSpec((width, cols), lambda i, *_: (0, 0)),
                pl.BlockSpec(q.shape, lambda i, *_: (0, 0)),
            ],
            out_specs=[
                pl.BlockSpec((per, rows, cols), lambda i, *_: (i, 0, 0)),
                pl.BlockSpec((PEERS * 2, 4, 128), lambda i, *_: (0, 0, 0)),
                pl.BlockSpec((2, 128, 256), lambda i, *_: (0, 0, 0)),
            ],
        ),
        out_shape=[
            jax.ShapeDtypeStruct((blocks, rows, cols), BF16),
            jax.ShapeDtypeStruct((PEERS * 2, 4, 128), F32),
            jax.ShapeDtypeStruct((2, 128, 256), BF16),
        ],
    )(owner, clip, valid, x, w, q)


def tops_kernel(mine_ref, all_ref, own_ref, inbox, send, recv, send2, recv2):
    sess, *_ = place()
    barrier = pltpu.get_barrier_semaphore()

    def signal(k, _):
        pl.semaphore_signal(
            barrier, inc=1, device_id={"sess": lax.rem(sess + k, PEERS)}, device_id_type=MESH
        )
        return _

    lax.fori_loop(1, PEERS, signal, 0)
    pl.semaphore_wait(barrier, PEERS - 1)

    def copy_in(k):
        to = lax.rem(sess + k, PEERS)
        return remote(mine_ref.at[to], inbox.at[k], send.at[k], recv.at[k], {"sess": to})

    def copy_out(k):
        to = lax.rem(sess + k, PEERS)
        return remote(own_ref, all_ref.at[sess], send2.at[k], recv2.at[k], {"sess": to})

    def arrival(k):
        source = lax.rem(sess + PEERS - k, PEERS)
        return remote(own_ref, all_ref.at[source], send2.at[k], recv2.at[k], {"sess": source})

    def start(k, _):
        copy_in(k).start()
        return _

    lax.fori_loop(1, PEERS, start, 0)

    def gather(k, top):
        copy_in(k).wait_recv()
        return jnp.maximum(top, inbox[k])

    top = lax.fori_loop(1, PEERS, gather, mine_ref[sess])
    own_ref[...] = top

    def start2(k, _):
        copy_out(k).start()
        return _

    lax.fori_loop(1, PEERS, start2, 0)
    all_ref[sess] = top

    def finish(k, _):
        copy_in(k).wait_send()
        copy_out(k).wait_send()
        arrival(k).wait_recv()
        return _

    lax.fori_loop(1, PEERS, finish, 0)


def exchange_tops(tops):
    return pl.pallas_call(
        tops_kernel,
        name="tops",
        out_shape=[
            jax.ShapeDtypeStruct((PEERS, 2, 4, 128), F32),
            jax.ShapeDtypeStruct((2, 4, 128), F32),
        ],
        in_specs=[VMEM_SPEC],
        out_specs=[VMEM_SPEC, VMEM_SPEC],
        scratch_shapes=[pltpu.VMEM((PEERS, 2, 4, 128), F32)] + [pltpu.SemaphoreType.DMA((PEERS,))] * 4,
        compiler_params=pltpu.CompilerParams(collective_id=1, has_side_effects=True),
    )(tops.reshape(PEERS, 2, 4, 128))


SUB = 264


def weigh_kernel(per, owner, clip, valid, kv_ref, tops_ref, qt_ref, out_ref):
    step = pl.program_id(0)
    rows = kv_ref.shape[1]

    @pl.when(step == 0)
    def _():
        out_ref[...] = jnp.zeros_like(out_ref)

    row = lax.broadcasted_iota(jnp.int32, (rows, 1), 0)
    for i in range(per):
        block = step * per + i
        who = owner[block]
        y_hi, z, core = who // (NZ * NC), (who // NC) % NZ, who % NC
        slot = ((core * NZ + z) * NY + y_hi) * 2 + clip[block]
        live = row < valid[block]
        for pair in range(2):
            scores = jnp.dot(
                kv_ref[i, :, pair * 128 : (pair + 1) * 128], qt_ref[pair], preferred_element_type=F32
            )
            values = kv_ref[i, :, 256 + pair * 128 : 256 + (pair + 1) * 128].astype(F32).T.astype(BF16)
            for inner in range(2):
                kh = pair * 2 + inner
                top = tops_ref[who * 2 + clip[block], kh : kh + 1, :]
                prob = jnp.where(live, jnp.exp(scores[:, inner * 128 : (inner + 1) * 128] - top), 0.0)
                total = jnp.sum(prob, axis=0, keepdims=True)
                part = jnp.dot(
                    values[inner * HEAD_DIM : (inner + 1) * HEAD_DIM, :],
                    prob.astype(BF16),
                    preferred_element_type=F32,
                )
                out_ref[slot, kh * HEAD_DIM : (kh + 1) * HEAD_DIM, :] += part
                out_ref[slot, 256 + kh : 257 + kh, :] += total


def weigh(owner, clip, valid, kv, tops, qt):
    blocks, rows, cols = kv.shape
    per = 2
    return pl.pallas_call(
        lambda *refs: weigh_kernel(per, *refs),
        name="weigh",
        grid_spec=pltpu.PrefetchScalarGridSpec(
            num_scalar_prefetch=3,
            grid=(blocks // per,),
            in_specs=[
                pl.BlockSpec((per, rows, cols), lambda i, *_: (i, 0, 0)),
                pl.BlockSpec((PEERS * 2, 4, 128), lambda i, *_: (0, 0, 0)),
                pl.BlockSpec((2, 128, 256), lambda i, *_: (0, 0, 0)),
            ],
            out_specs=pl.BlockSpec((PEERS * 2, SUB, 128), lambda i, *_: (0, 0, 0)),
        ),
        out_shape=jax.ShapeDtypeStruct((PEERS * 2, SUB, 128), F32),
    )(owner, clip, valid, kv, tops, qt)


ORDER = (4, 3, 5, 2, 6, 1, 7, 0)


CODE_TOP = 32767.0


def encode(value, code_ref, meta_ref, at):
    for kh in range(KV_HEADS):
        part = value[kh * HEAD_DIM : (kh + 1) * HEAD_DIM]
        largest = jnp.maximum(jnp.max(jnp.abs(part), axis=0, keepdims=True), 1e-30)
        code = jnp.round(part * (CODE_TOP / largest)).astype(jnp.int32).astype(jnp.int16)
        code_ref[at + (slice(kh * HEAD_DIM, (kh + 1) * HEAD_DIM), slice(None))] = code
        meta_ref[at + (slice(4 + kh, 5 + kh), slice(None))] = largest * (1.0 / CODE_TOP)
    meta_ref[at + (slice(0, 4), slice(None))] = value[256:260]


def decode(code_ref, meta_ref, at):
    parts = []
    for kh in range(KV_HEADS):
        code = code_ref[at + (slice(kh * HEAD_DIM, (kh + 1) * HEAD_DIM), slice(None))].astype(jnp.int32).astype(F32)
        parts.append(code * meta_ref[at + (slice(4 + kh, 5 + kh), slice(None))])
    return parts, meta_ref[at + (slice(0, 4), slice(None))]


def plus(value, decoded):
    parts, totals = decoded
    tail = jnp.concatenate([totals, jnp.zeros((4, 128), F32)], axis=0)
    return value + jnp.concatenate(parts + [tail], axis=0)


def reduce_kernel(
    part_ref, wo_ref, wp_ref, out_ref, wo_out, wp_out,
    twin_in, run, run_meta, chain_in, chain_meta, y_out, y_out_meta, y_in, y_meta,
    csend, crecv, zsend, zrecv, msend, mrecv, ysend, yrecv, wsend, wrecv, local,
):
    sess, y_hi, z, core = place()
    half, _, near, far, twin = weight_peers()
    up = {"sess": sess_of(y_hi, lax.rem(z + 1, NZ), core)}
    down = {"sess": sess_of(y_hi, lax.rem(z + NZ - 1, NZ), core)}
    across = {"sess": sess_of(1 - y_hi, z, core)}
    barrier = pltpu.get_barrier_semaphore()
    for to in (near, far, twin, up, down, across):
        pl.semaphore_signal(barrier, inc=1, device_id=to, device_id_type=MESH)
    owns = [
        pltpu.make_async_copy(wo_ref, wo_out.at[half], local.at[0]),
        pltpu.make_async_copy(wp_ref, wp_out.at[half], local.at[1]),
    ]
    for c in owns:
        c.start()
    pl.semaphore_wait(barrier, 6)

    to_twin = {}
    for k in ORDER:
        dest = lax.rem(z + k, NZ)
        to_twin[k] = remote(part_ref.at[1 - core, dest], twin_in.at[k], csend.at[k], crecv.at[k], twin)
        to_twin[k].start()
    weights = []
    for i, (src, out) in enumerate(((wo_ref, wo_out), (wp_ref, wp_out))):
        weights.append(weight_copies(src, out, wsend.at[i], wrecv.at[i]))
        for c in weights[i][0]:
            c.start()

    sent = {}
    ways = (up, down)

    def own_sum(k, sub):
        return part_ref[core, lax.rem(z + k, NZ), sub] + twin_in[k, sub]

    def pass_on(way, hop, sub, value):
        at = (way, hop, sub)
        encode(value, run, run_meta, at)
        sent[at] = [
            remote(run.at[at], chain_in.at[at], zsend.at[at], zrecv.at[at], ways[way]),
            remote(run_meta.at[at], chain_meta.at[at], msend.at[at], mrecv.at[at], ways[way]),
        ]
        for c in sent[at]:
            c.start()

    def arrived(way, hop, sub):
        for c in sent[way, hop, sub]:
            c.wait_recv()
        return decode(chain_in, chain_meta, (way, hop, sub))

    to_twin[4].wait_recv()
    for sub in range(2):
        pass_on(0, 0, sub, own_sum(4, sub))
        pass_on(1, 0, 2 + sub, own_sum(4, 2 + sub))
    for hop in range(1, 4):
        ks = (4 - hop, NZ - (4 - hop))
        for k in ks:
            to_twin[k].wait_recv()
        for turn in range(4):
            for way in range(2):
                sub = (turn + 2) % 4 if way == 0 else turn
                value = own_sum(ks[way], sub)
                if (way, hop - 1, sub) in sent:
                    value = plus(value, arrived(way, hop - 1, sub))
                pass_on(way, hop, sub, value)
        if hop == 1:
            for first, relay in weights:
                for c, r in zip(first, relay):
                    c.wait_recv()
                    r.start()

    to_twin[0].wait_recv()

    def total_here(y, i):
        sub = y * 2 + i
        value = own_sum(0, sub)
        for way in range(2):
            value = plus(value, decode(chain_in, chain_meta, (way, 3, sub)))
        return value

    for sub in range(4):
        for way in range(2):
            for c in sent[way, 3, sub]:
                c.wait_recv()
    over = []
    for i in range(2):
        encode(total_here(1 - y_hi, i), y_out, y_out_meta, (i,))
        pair = [
            remote(y_out.at[i], y_in.at[i], ysend.at[i, 0], yrecv.at[i, 0], across),
            remote(y_out_meta.at[i], y_meta.at[i], ysend.at[i, 1], yrecv.at[i, 1], across),
        ]
        for c in pair:
            c.start()
        over.append(pair)
    mine = [total_here(y_hi, i) for i in range(2)]
    for i in range(2):
        for c in over[i]:
            c.wait_recv()
        out_ref[i] = plus(mine[i], decode(y_in, y_meta, (i,)))

    for c in [c for pair in over for c in pair] + [c for pair in sent.values() for c in pair]:
        c.wait_send()
    for c in to_twin.values():
        c.wait_send()
    for first, relay in weights:
        for r in relay:
            r.wait_recv()
        for c in first + relay:
            c.wait_send()
    for c in owns:
        c.wait()


def reduce_to_owner(parts, w_out, w_proj):
    wo = w_out.reshape(4, w_out.shape[0] // 4, w_out.shape[1])
    wp = w_proj.reshape(4, w_proj.shape[0] // 4, w_proj.shape[1])
    dma = pltpu.SemaphoreType.DMA
    sums, wo_all, wp_all = pl.pallas_call(
        reduce_kernel,
        name="reduce",
        out_shape=[
            jax.ShapeDtypeStruct((2, SUB, 128), F32),
            jax.ShapeDtypeStruct((2,) + wo.shape, wo.dtype),
            jax.ShapeDtypeStruct((2,) + wp.shape, wp.dtype),
        ],
        in_specs=[VMEM_SPEC] * 3,
        out_specs=[VMEM_SPEC] * 3,
        scratch_shapes=[
            pltpu.VMEM((NZ, 4, SUB, 128), F32),
            pltpu.VMEM((2, 4, 4, 256, 128), jnp.int16),
            pltpu.VMEM((2, 4, 4, 8, 128), F32),
            pltpu.VMEM((2, 4, 4, 256, 128), jnp.int16),
            pltpu.VMEM((2, 4, 4, 8, 128), F32),
            pltpu.VMEM((2, 256, 128), jnp.int16),
            pltpu.VMEM((2, 8, 128), F32),
            pltpu.VMEM((2, 256, 128), jnp.int16),
            pltpu.VMEM((2, 8, 128), F32),
            dma((NZ,)),
            dma((NZ,)),
            dma((2, 4, 4)),
            dma((2, 4, 4)),
            dma((2, 4, 4)),
            dma((2, 4, 4)),
            dma((2, 2)),
            dma((2, 2)),
            dma((2, 4)),
            dma((2, 4)),
            dma((2,)),
        ],
        compiler_params=pltpu.CompilerParams(collective_id=2, has_side_effects=True),
    )(parts.reshape(NC, NZ, NY * 2, SUB, 128), wo, wp)
    return sums, wo_all.reshape(-1, w_out.shape[1]), wp_all.reshape(-1, w_proj.shape[1])


def embed_kernel(
    frame, scale, sums_ref, top_ref, lat_ref, wo_ref, wp_ref, movie_ref, state_ref, msg_ref, logit_ref, pick_ref, attn
):
    lat = lat_ref.shape[0]
    for c in range(2):
        columns = []
        for kh in range(KV_HEADS):
            total = sums_ref[c, 256 + kh : 257 + kh, :] + jnp.exp(-top_ref[c, kh : kh + 1, :])
            columns.append(sums_ref[c, kh * HEAD_DIM : (kh + 1) * HEAD_DIM, :] / total)
        turned = jnp.concatenate(columns, axis=0).T.astype(BF16)
        for head in range(HEADS):
            kh, j = head // GROUP, head % GROUP
            attn[c * lat : (c + 1) * lat, head * HEAD_DIM : (head + 1) * HEAD_DIM] = turned[
                j * lat : (j + 1) * lat, kh * HEAD_DIM : (kh + 1) * HEAD_DIM
            ]
    mixed = jnp.dot(attn[...], wo_ref[...], preferred_element_type=F32)
    row = lax.broadcasted_iota(jnp.int32, (16, 1), 0)
    pooled = jnp.zeros((16, mixed.shape[1]), F32)
    for c in range(2):
        state = lat_ref[...].astype(F32) + mixed[c * lat : (c + 1) * lat]
        state_ref[c] = state.astype(BF16)
        pooled = jnp.where(row == c, jnp.mean(state, axis=0, keepdims=True), pooled)
    z = jnp.dot(pooled.astype(BF16), wp_ref[...], preferred_element_type=F32)
    zn = (z / jnp.sqrt(jnp.sum(z * z, axis=-1, keepdims=True) + 1e-06)).astype(BF16)
    movie = movie_ref[...].astype(F32)
    tn = (movie / jnp.sqrt(jnp.sum(movie * movie, axis=-1, keepdims=True) + 1e-06)).astype(BF16)
    logits = lax.dot_general(zn, tn, (((1,), (1,)), ((), ())), preferred_element_type=F32) * scale[0]
    lane = lax.broadcasted_iota(jnp.int32, (1, 128), 1)
    for r in range(4):
        piece = logits[:, r * 128 : (r + 1) * 128]
        msg_ref[r : r + 1, :] = jnp.exp(piece[0:1]) + jnp.exp(piece[1:2])
        picks = []
        for c in range(2):
            picks.append((lane + r * 128 == frame[c]).astype(F32))
            logit_ref[c * 4 + r : c * 4 + r + 1, :] = piece[c : c + 1]
            pick_ref[c * 4 + r : c * 4 + r + 1, :] = picks[c]
        msg_ref[4 + r : 5 + r, :] = picks[0] + picks[1]


def embed(frame, scale, sums, top, latents, w_out, w_proj, movie):
    lat, width = latents.shape
    small = jax.ShapeDtypeStruct((8, 128), F32)
    return pl.pallas_call(
        embed_kernel,
        name="embed",
        out_shape=[jax.ShapeDtypeStruct((2, lat, width), BF16), small, small, small],
        in_specs=[SMEM_SPEC, SMEM_SPEC] + [VMEM_SPEC] * 6,
        out_specs=[VMEM_SPEC] * 4,
        scratch_shapes=[pltpu.VMEM((2 * lat, width), BF16)],
    )(frame, scale, sums, top, latents, w_out, w_proj, movie)


def loss_kernel(msg_ref, logit_ref, pick_ref, out_ref, inbox, inbox2, column, send, recv, send2, recv2):
    sess, y_hi, z, core = place()
    x, half = lax.axis_index("dp"), lax.axis_index("fsdp")
    spots = NY * NC * 4 * 2
    here = ((y_hi * NC + core) * 4 + x) * 2 + half

    def along(k):
        return {"sess": sess_of(y_hi, lax.rem(z + k, NZ), core)}

    def plane(k):
        at = lax.rem(here + k, spots)
        return {
            "sess": sess_of(at // (NC * 8), z, (at // 8) % NC),
            "dp": (at // 2) % 4,
            "fsdp": at % 2,
        }

    barrier = pltpu.get_barrier_semaphore()

    def signal_z(k, _):
        pl.semaphore_signal(barrier, inc=1, device_id=along(k), device_id_type=MESH)
        return _

    def signal_p(k, _):
        pl.semaphore_signal(barrier, inc=1, device_id=plane(k), device_id_type=MESH)
        return _

    lax.fori_loop(1, NZ, signal_z, 0)
    lax.fori_loop(1, spots, signal_p, 0)
    pl.semaphore_wait(barrier, NZ - 1 + spots - 1)

    def copy_z(k):
        return remote(msg_ref, inbox.at[k], send.at[k], recv.at[k], along(k))

    def copy_p(k):
        return remote(column, inbox2.at[k], send2.at[k], recv2.at[k], plane(k))

    def start_z(k, _):
        copy_z(k).start()
        return _

    def add_z(k, total):
        copy_z(k).wait_recv()
        return total + inbox[k]

    def start_p(k, _):
        copy_p(k).start()
        return _

    def add_p(k, total):
        copy_p(k).wait_recv()
        return total + inbox2[k]

    lax.fori_loop(1, NZ, start_z, 0)
    total = lax.fori_loop(1, NZ, add_z, msg_ref[...])
    column[...] = total
    lax.fori_loop(1, spots, start_p, 0)
    total = lax.fori_loop(1, spots, add_p, total)

    def whole(v):
        return jnp.sum(jnp.sum(v, axis=1, keepdims=True), axis=0, keepdims=True)

    for c in range(2):
        logit, pick = logit_ref[c * 4 : c * 4 + 4, :], pick_ref[c * 4 : c * 4 + 4, :]
        row_sum = whole(total[4:8] * jnp.exp(logit))
        col_sum = whole(total[0:4] * pick)
        loss = 0.5 * (jnp.log(row_sum) + jnp.log(col_sum)) - whole(logit * pick)
        out_ref[c : c + 1, :] = jnp.broadcast_to(loss, (1, 128))

    def end_z(k, _):
        copy_z(k).wait_send()
        return _

    def end_p(k, _):
        copy_p(k).wait_send()
        return _

    lax.fori_loop(1, NZ, end_z, 0)
    lax.fori_loop(1, spots, end_p, 0)


def clip_losses(msg, logits, picks):
    dma = pltpu.SemaphoreType.DMA
    spots = NY * NC * 8
    return pl.pallas_call(
        loss_kernel,
        name="loss",
        out_shape=jax.ShapeDtypeStruct((2, 128), F32),
        in_specs=[VMEM_SPEC] * 3,
        out_specs=VMEM_SPEC,
        scratch_shapes=[
            pltpu.VMEM((NZ, 8, 128), F32),
            pltpu.VMEM((spots, 8, 128), F32),
            pltpu.VMEM((8, 128), F32),
            dma((NZ,)),
            dma((NZ,)),
            dma((spots,)),
            dma((spots,)),
        ],
        compiler_params=pltpu.CompilerParams(collective_id=3, has_side_effects=True),
    )(msg, logits, picks)


def per_device(
    unit_tokens,
    block_owner,
    block_clip,
    block_valid,
    latent_query_rows,
    latents,
    w_kv,
    w_out,
    w_proj,
    movie_frame_embeddings,
    clip_frame,
    logit_scale,
):
    owner = block_owner.reshape(-1)
    weight = gather_kv_weight(w_kv)
    kv, tops, qt = project(owner, block_clip, block_valid, unit_tokens, weight, latent_query_rows)
    all_tops, own_top = exchange_tops(tops)
    parts = weigh(owner, block_clip, block_valid, kv, all_tops.reshape(PEERS * 2, 4, 128), qt)
    sums, wo, wp = reduce_to_owner(parts, w_out, w_proj)
    state, msg, logits, picks = embed(
        clip_frame, logit_scale, sums, own_top, latents, wo, wp, movie_frame_embeddings
    )
    loss = clip_losses(msg, logits, picks)
    return state, loss[:, 0]


def solution(mesh):
    return jax.shard_map(
        per_device,
        mesh=mesh,
        in_specs=(
            P(("sess", "dp", "fsdp"), None, None),
            P(("sess", "dp", "fsdp"), None),
            P(("sess", "dp", "fsdp")),
            P(("sess", "dp", "fsdp")),
            P(),
            P(),
            P("fsdp", None),
            P("fsdp", None),
            P("fsdp", None),
            P(),
            P(("sess", "dp", "fsdp")),
            P(),
        ),
        out_specs=(P(("sess", "dp", "fsdp"), None, None), P(("sess", "dp", "fsdp"))),
        check_vma=False,
    )
```

```python
import jax
import jax.numpy as jnp
from jax import lax
from jax.experimental import pallas as pl
from jax.experimental.pallas import tpu as pltpu
from jax.sharding import PartitionSpec as P

HEADS = 16
HEAD_DIM = 64
KV_HEADS = 4
GROUP = HEADS // KV_HEADS
NZ = 8
NY = 2
NC = 2
NX = 4
PEERS = NY * NZ * NC
SPOTS = NY * NC * NX * 2
SUB = 264
PER = 2
ORDER = (4, 3, 5, 2, 6, 1, 7, 0)
F32 = jnp.float32
BF16 = jnp.bfloat16
MESH = pl.DeviceIdType.MESH
VMEM_SPEC = pl.BlockSpec(memory_space=pltpu.VMEM)
SMEM_SPEC = pl.BlockSpec(memory_space=pltpu.SMEM)
ANY_SPEC = pl.BlockSpec(memory_space=pl.ANY)


def place():
    sess = lax.axis_index("sess")
    y_hi = sess // (NZ * NC)
    z = (sess // NC) % NZ
    core = sess % NC
    return sess, y_hi, z, core


def sess_of(y_hi, z, core):
    return (y_hi * NZ + z) * NC + core


def remote(src, dst, send_sem, recv_sem, where):
    return pltpu.make_async_remote_copy(
        src_ref=src, dst_ref=dst, send_sem=send_sem, recv_sem=recv_sem, device_id=where, device_id_type=MESH
    )


def each(first, last, do):
    def step(k, carry):
        do(k)
        return carry

    lax.fori_loop(first, last, step, 0)


CODE_TOP = 32767.0


def head_rows(kh):
    return slice(kh * HEAD_DIM, (kh + 1) * HEAD_DIM)


def whole_part(ref, *at):
    return [
        (ref[at + (head_rows(kh),)], None, ref[at + (slice(256 + kh, 257 + kh),)], ref[at + (slice(260 + kh, 261 + kh),)])
        for kh in range(KV_HEADS)
    ]


def coded_part(code_ref, meta_ref, *at):
    out = []
    for kh in range(KV_HEADS):
        code = code_ref[at + (head_rows(kh),)].astype(jnp.int32).astype(F32)
        scale, total, top = (meta_ref[at + (slice(i * 4 + kh, i * 4 + kh + 1),)] for i in range(3))
        out.append((code, scale, total, top))
    return out


def merge(*parts):
    out = []
    for heads in zip(*parts):
        top = heads[0][3]
        for head in heads[1:]:
            top = jnp.maximum(top, head[3])
        sums = total = None
        for values, scale, part_total, part_top in heads:
            factor = jnp.exp(part_top - top)
            total = part_total * factor if total is None else total + part_total * factor
            term = values * (factor if scale is None else factor * scale)
            sums = term if sums is None else sums + term
        out.append((sums, None, total, top))
    return out


def keep(part, ref, *at):
    for kh, (values, _, total, top) in enumerate(part):
        ref[at + (head_rows(kh),)] = values
        ref[at + (slice(256 + kh, 257 + kh),)] = total
        ref[at + (slice(260 + kh, 261 + kh),)] = top


def encode(part, code_ref, meta_ref, *at):
    for kh, (values, _, total, top) in enumerate(part):
        largest = jnp.maximum(jnp.max(jnp.abs(values), axis=0, keepdims=True), 1e-30)
        code = jnp.round(values * (CODE_TOP / largest)).astype(jnp.int32).astype(jnp.int16)
        code_ref[at + (head_rows(kh),)] = code
        for i, line in enumerate((largest * (1.0 / CODE_TOP), total, top)):
            meta_ref[at + (slice(i * 4 + kh, i * 4 + kh + 1),)] = line


def kernel(
    owner, clip, valid, frame,
    x_any, wkv_any, q_ref, lat_ref, scale, wo_any, wp_any, movie_any,
    state_ref, loss_ref,
    x_ref, wkv, wo, wp, movie, tn, qt, acc, table_rows, table,
    part, twin_out, twin_in, run, run_meta, chain_in, chain_meta, y_out, y_out_meta, y_in, y_meta, sums, attn,
    msg, logit_ref, pick_ref, column, inbox_z, inbox_p,
    xsem, local, ksend, krecv, wsend, wrecv,
    csend, crecv, zsend, zrecv, msend, mrecv, ysend, yrecv, lzsend, lzrecv, lpsend, lprecv,
):
    sess, y_hi, z, core = place()
    x, half = lax.axis_index("dp"), lax.axis_index("fsdp")
    blocks, rows, width = x_ref.shape
    lat = lat_ref.shape[0]
    groups = blocks // PER
    half_width = width // 2
    near = {"sess": sess, "fsdp": 1 - half}
    far = {"sess": sess_of(1 - y_hi, z, core), "fsdp": 1 - half}
    twin = {"sess": sess_of(y_hi, z, 1 - core)}
    up = {"sess": sess_of(y_hi, lax.rem(z + 1, NZ), core)}
    down = {"sess": sess_of(y_hi, lax.rem(z + NZ - 1, NZ), core)}
    across = {"sess": sess_of(1 - y_hi, z, core)}
    here = ((y_hi * NC + core) * NX + x) * 2 + half

    def along(k):
        return {"sess": sess_of(y_hi, lax.rem(z + k, NZ), core)}

    def plane(k):
        at = lax.rem(here + k, SPOTS)
        return {"sess": sess_of(at // (NC * NX * 2), z, (at // (NX * 2)) % NC), "dp": (at // 2) % NX, "fsdp": at % 2}

    barrier = pltpu.get_barrier_semaphore()

    def greet(to):
        pl.semaphore_signal(barrier, inc=1, device_id=to, device_id_type=MESH)

    each(1, SPOTS, lambda k: greet(plane(k)))
    each(1, NZ, lambda k: greet(along(k)))
    own_w = pltpu.make_async_copy(wkv_any, wkv.at[half], local.at[0])
    own_w.start()

    def load_x(g):
        at = pl.ds(g * PER, PER)
        return pltpu.make_async_copy(x_any.at[at], x_ref.at[at], xsem.at[g])

    each(0, groups, lambda g: load_x(g).start())
    load_movie = pltpu.make_async_copy(movie_any, movie, local.at[1])
    load_movie.start()
    own_wo = pltpu.make_async_copy(wo_any, wo.at[half], local.at[2])
    own_wp = pltpu.make_async_copy(wp_any, wp.at[half], local.at[3])
    own_wo.start()
    own_wp.start()
    own_w.wait()
    w_here = wkv[half].reshape(half_width, wkv.shape[3])
    here_at = pl.ds(pl.multiple_of(half * half_width, half_width), half_width)
    there_at = pl.ds(pl.multiple_of((1 - half) * half_width, half_width), half_width)

    def project_here(g):
        load_x(g).wait()
        xs = x_ref[pl.ds(g * PER, PER), :, here_at].reshape(PER * rows, half_width)
        acc[g] = jnp.dot(xs, w_here, preferred_element_type=F32)

    each(0, groups, project_here)

    pl.semaphore_wait(barrier, SPOTS + NZ - 2)

    def weight_copies(src, out, send, recv):
        first = [
            remote(src.at[2 * core + i], out.at[half, 2 * core + i], send.at[i], recv.at[i], to)
            for i, to in enumerate((near, far))
        ]
        relay = [
            remote(
                out.at[1 - half, 2 * core + i], out.at[1 - half, 2 * core + i], send.at[2 + i], recv.at[2 + i], twin
            )
            for i in range(2)
        ]
        return first, relay

    kv_first, kv_relay = weight_copies(wkv_any, wkv, ksend, krecv)
    for c in kv_first:
        c.start()

    qt[...] = jnp.zeros_like(qt)
    turned = (q_ref[...].astype(F32) * (HEAD_DIM**-0.5)).T.astype(BF16)
    for head in range(HEADS):
        kh, j = head // GROUP, head % GROUP
        pair, inner = kh // 2, kh % 2
        left = inner * GROUP * lat + j * lat
        qt[pair, inner * HEAD_DIM : (inner + 1) * HEAD_DIM, left : left + lat] = turned[
            head * HEAD_DIM : (head + 1) * HEAD_DIM, :
        ]
    part[blocks] = jnp.zeros((SUB, 128), F32)
    lane = lax.broadcasted_iota(jnp.int32, (8, 128), 1)
    lines = jnp.full((8, 128), blocks * 2, jnp.int32)
    for block in range(blocks):
        who = owner[block]
        slot = (who % NC) * (NZ * NY * 2) + (who // NC % NZ) * (NY * 2) + who // (NZ * NC) * 2 + clip[block]
        counted = jnp.where(lane < PEERS * 2, block, blocks - 1 - block)
        lines = jnp.minimum(lines, jnp.where(lane % (PEERS * 2) == slot, counted, blocks * 2))
    table_rows[...] = lines
    load_table = pltpu.make_async_copy(table_rows, table, local.at[4])
    load_table.start()
    load_movie.wait()
    frames = movie[...].astype(F32)
    tn[...] = (frames / jnp.sqrt(jnp.sum(frames * frames, axis=-1, keepdims=True) + 1e-06)).astype(BF16)

    for c, r in zip(kv_first, kv_relay):
        c.wait_recv()
        r.start()
    for r in kv_relay:
        r.wait_recv()

    weights = [weight_copies(wo_any, wo, wsend.at[0], wrecv.at[0]), weight_copies(wp_any, wp, wsend.at[1], wrecv.at[1])]
    for first, _ in weights:
        for c in first:
            c.start()

    w_there = wkv[1 - half].reshape(half_width, wkv.shape[3])
    row = lax.broadcasted_iota(jnp.int32, (rows, 1), 0)

    def project_there(g):
        xs = x_ref[pl.ds(g * PER, PER), :, there_at].reshape(PER * rows, half_width)
        kv = (acc[g] + jnp.dot(xs, w_there, preferred_element_type=F32)).astype(BF16)
        for pair in range(2):
            both = jnp.dot(kv[:, pair * 128 : (pair + 1) * 128], qt[pair], preferred_element_type=F32)
            for i in range(PER):
                block = g * PER + i
                piece = both[i * rows : (i + 1) * rows, :]
                live = row < valid[block]
                top = jnp.max(jnp.where(live, piece, 0.0), axis=0, keepdims=True)
                prob = jnp.where(live, jnp.exp(piece - top), 0.0)
                total = jnp.sum(prob, axis=0, keepdims=True)
                rounded = prob.astype(BF16)
                values = kv[i * rows : (i + 1) * rows, 256 + pair * 128 : 256 + (pair + 1) * 128]
                values = values.astype(F32).T.astype(BF16)
                for inner in range(2):
                    kh = pair * 2 + inner
                    columns = slice(inner * 128, (inner + 1) * 128)
                    part[block, head_rows(kh), :] = jnp.dot(
                        values[head_rows(inner), :], rounded[:, columns], preferred_element_type=F32
                    )
                    part[block, 256 + kh : 257 + kh, :] = total[:, columns]
                    part[block, 260 + kh : 261 + kh, :] = top[:, columns]

    each(0, groups, project_there)
    load_table.wait()

    def local_parts(core_to, z_to, turn):
        sub = lax.rem(turn + 2 * (1 - y_hi), 4)
        slot = (core_to * NZ + z_to) * (NY * 2) + sub
        one = jnp.minimum(table[0, slot], blocks)
        two = blocks - 1 - table[0, PEERS * 2 + slot]
        two = jnp.where(two > one, two, blocks)
        return whole_part(part, one), whole_part(part, two)

    to_twin = {}
    for k in ORDER:
        dest = lax.rem(z + k, NZ)
        for turn in range(4):
            keep(merge(*local_parts(1 - core, dest, turn)), twin_out, k, turn)
        to_twin[k] = remote(twin_out.at[k], twin_in.at[k], csend.at[k], crecv.at[k], twin)
        to_twin[k].start()

    sent = {}
    ways = (up, down)

    def own_parts(k, turn):
        return local_parts(core, lax.rem(z + k, NZ), turn) + (whole_part(twin_in, k, turn),)

    def pass_on(way, hop, turn, *parts):
        at = (way, hop, turn)
        encode(merge(*parts), run, run_meta, *at)
        sent[at] = [
            remote(run.at[at], chain_in.at[at], zsend.at[at], zrecv.at[at], ways[way]),
            remote(run_meta.at[at], chain_meta.at[at], msend.at[at], mrecv.at[at], ways[way]),
        ]
        for c in sent[at]:
            c.start()

    def arrived(way, hop, turn):
        for c in sent[way, hop, turn]:
            c.wait_recv()
        return coded_part(chain_in, chain_meta, way, hop, turn)

    to_twin[4].wait_recv()
    for i in range(2):
        pass_on(0, 0, 2 + i, *own_parts(4, 2 + i))
        pass_on(1, 0, i, *own_parts(4, i))
    turns = {1: ((0, 1, 2, 3), (2, 0, 3, 1)), 2: ((0, 1, 2, 3), (0, 2, 1, 3)), 3: ((0, 1, 2, 3), (0, 1, 2, 3))}
    for hop in range(1, 4):
        ks = (4 - hop, NZ - (4 - hop))
        for k in ks:
            to_twin[k].wait_recv()
        for place_at in range(4):
            for way in range(2):
                turn = turns[hop][way][place_at]
                parts = own_parts(ks[way], turn)
                if (way, hop - 1, turn) in sent:
                    parts = parts + (arrived(way, hop - 1, turn),)
                pass_on(way, hop, turn, *parts)
        if hop == 1:
            for first, relay in weights:
                for c, r in zip(first, relay):
                    c.wait_recv()
                    r.start()

    to_twin[0].wait_recv()

    def here_parts(turn):
        return own_parts(0, turn) + (arrived(0, 3, turn), arrived(1, 3, turn))

    over = []
    for i in range(2):
        encode(merge(*here_parts(i)), y_out, y_out_meta, i)
        pair = [
            remote(y_out.at[i], y_in.at[i], ysend.at[i, 0], yrecv.at[i, 0], across),
            remote(y_out_meta.at[i], y_meta.at[i], ysend.at[i, 1], yrecv.at[i, 1], across),
        ]
        for c in pair:
            c.start()
        over.append(pair)
    for i in range(2):
        keep(merge(*here_parts(2 + i)), sums, i)
    for _, relay in weights:
        for r in relay:
            r.wait_recv()
    own_wo.wait()
    own_wp.wait()

    for c in range(2):
        for copy in over[c]:
            copy.wait_recv()
        columns = []
        for values, _, total, top in merge(whole_part(sums, c), coded_part(y_in, y_meta, c)):
            columns.append(values / (total + jnp.exp(-top)))
        flat = jnp.concatenate(columns, axis=0).T.astype(BF16)
        for head in range(HEADS):
            kh, j = head // GROUP, head % GROUP
            attn[c * lat : (c + 1) * lat, head * HEAD_DIM : (head + 1) * HEAD_DIM] = flat[
                j * lat : (j + 1) * lat, kh * HEAD_DIM : (kh + 1) * HEAD_DIM
            ]
    mixed = jnp.dot(attn[...], wo[...].reshape(width, width), preferred_element_type=F32)
    row16 = lax.broadcasted_iota(jnp.int32, (16, 1), 0)
    pooled = jnp.zeros((16, width), F32)
    for c in range(2):
        state = lat_ref[...].astype(F32) + mixed[c * lat : (c + 1) * lat]
        state_ref[c] = state.astype(BF16)
        pooled = jnp.where(row16 == c, jnp.mean(state, axis=0, keepdims=True), pooled)
    embed = jnp.dot(pooled.astype(BF16), wp[...].reshape(width, wp.shape[3]), preferred_element_type=F32)
    zn = (embed / jnp.sqrt(jnp.sum(embed * embed, axis=-1, keepdims=True) + 1e-06)).astype(BF16)
    logits = lax.dot_general(zn, tn[...], (((1,), (1,)), ((), ())), preferred_element_type=F32) * scale[...]
    lane = lax.broadcasted_iota(jnp.int32, (1, 128), 1)
    for r in range(4):
        piece = logits[:, r * 128 : (r + 1) * 128]
        msg[r : r + 1, :] = jnp.exp(piece[0:1]) + jnp.exp(piece[1:2])
        picks = []
        for c in range(2):
            picks.append((lane + r * 128 == frame[c]).astype(F32))
            logit_ref[c * 4 + r : c * 4 + r + 1, :] = piece[c : c + 1]
            pick_ref[c * 4 + r : c * 4 + r + 1, :] = picks[c]
        msg[4 + r : 5 + r, :] = picks[0] + picks[1]

    def sum_z(k):
        return remote(msg, inbox_z.at[k], lzsend.at[k], lzrecv.at[k], along(k))

    def sum_p(k):
        return remote(column, inbox_p.at[k], lpsend.at[k], lprecv.at[k], plane(k))

    def add_z(k, total):
        sum_z(k).wait_recv()
        return total + inbox_z[k]

    def add_p(k, total):
        sum_p(k).wait_recv()
        return total + inbox_p[k]

    each(1, NZ, lambda k: sum_z(k).start())
    total = lax.fori_loop(1, NZ, add_z, msg[...])
    column[...] = total
    each(1, SPOTS, lambda k: sum_p(k).start())

    for c in kv_first + kv_relay:
        c.wait_send()
    for c in [c for pair in over for c in pair] + [c for pair in sent.values() for c in pair]:
        c.wait_send()
    for c in to_twin.values():
        c.wait_send()
    for first, relay in weights:
        for c in first + relay:
            c.wait_send()
    each(1, NZ, lambda k: sum_z(k).wait_send())

    total = lax.fori_loop(1, SPOTS, add_p, total)

    def whole(v):
        return jnp.sum(jnp.sum(v, axis=1, keepdims=True), axis=0, keepdims=True)

    for c in range(2):
        logit, pick = logit_ref[c * 4 : c * 4 + 4, :], pick_ref[c * 4 : c * 4 + 4, :]
        row_sum = whole(total[4:8] * jnp.exp(logit))
        col_sum = whole(total[0:4] * pick)
        loss = 0.5 * (jnp.log(row_sum) + jnp.log(col_sum)) - whole(logit * pick)
        loss_ref[c : c + 1, :] = jnp.broadcast_to(loss, (1, 128))
    each(1, SPOTS, lambda k: sum_p(k).wait_send())


def output_kernel(state_in, loss_in, state_ref, loss_ref):
    state_ref[...] = state_in[...]
    for c in range(2):
        loss_ref[c] = jnp.max(loss_in[c : c + 1, :])


def per_device(
    unit_tokens,
    block_owner,
    block_clip,
    block_valid,
    latent_query_rows,
    latents,
    w_kv,
    w_out,
    w_proj,
    movie_frame_embeddings,
    clip_frame,
    logit_scale,
):
    owner = block_owner.reshape(-1)
    blocks, rows, width = unit_tokens.shape
    cols = w_kv.shape[1]
    dma = pltpu.SemaphoreType.DMA
    vmem = pltpu.VMEM
    i16 = jnp.int16

    def quarters(w):
        return w.reshape(4, w.shape[0] // 4, w.shape[1])

    wkv, wo, wp = quarters(w_kv), quarters(w_out), quarters(w_proj)
    state, loss = pl.pallas_call(
        kernel,
        name="session",
        out_shape=[jax.ShapeDtypeStruct((2,) + latents.shape, BF16), jax.ShapeDtypeStruct((2, 128), F32)],
        in_specs=[SMEM_SPEC] * 4
        + [ANY_SPEC, ANY_SPEC, VMEM_SPEC, VMEM_SPEC, VMEM_SPEC, ANY_SPEC, ANY_SPEC, ANY_SPEC],
        out_specs=[VMEM_SPEC, VMEM_SPEC],
        scratch_shapes=[
            vmem(unit_tokens.shape, BF16),
            vmem((2,) + wkv.shape, BF16),
            vmem((2,) + wo.shape, BF16),
            vmem((2,) + wp.shape, BF16),
            vmem(movie_frame_embeddings.shape, BF16),
            vmem(movie_frame_embeddings.shape, BF16),
            vmem((2, 128, 256), BF16),
            vmem((blocks // PER, PER * rows, cols), F32),
            vmem((8, 128), jnp.int32),
            pltpu.SMEM((8, 128), jnp.int32),
            vmem((blocks + 1, SUB, 128), F32),
            vmem((NZ, 4, SUB, 128), F32),
            vmem((NZ, 4, SUB, 128), F32),
            vmem((2, 4, 4, 256, 128), i16),
            vmem((2, 4, 4, 12, 128), F32),
            vmem((2, 4, 4, 256, 128), i16),
            vmem((2, 4, 4, 12, 128), F32),
            vmem((2, 256, 128), i16),
            vmem((2, 12, 128), F32),
            vmem((2, 256, 128), i16),
            vmem((2, 12, 128), F32),
            vmem((2, SUB, 128), F32),
            vmem((2 * latents.shape[0], width), BF16),
            vmem((8, 128), F32),
            vmem((8, 128), F32),
            vmem((8, 128), F32),
            vmem((8, 128), F32),
            vmem((NZ, 8, 128), F32),
            vmem((SPOTS, 8, 128), F32),
            dma((blocks // PER,)),
            dma((5,)),
            dma((4,)),
            dma((4,)),
            dma((2, 4)),
            dma((2, 4)),
            dma((NZ,)),
            dma((NZ,)),
            dma((2, 4, 4)),
            dma((2, 4, 4)),
            dma((2, 4, 4)),
            dma((2, 4, 4)),
            dma((2, 2)),
            dma((2, 2)),
            dma((NZ,)),
            dma((NZ,)),
            dma((SPOTS,)),
            dma((SPOTS,)),
        ],
        compiler_params=pltpu.CompilerParams(collective_id=0, has_side_effects=True),
    )(
        owner,
        block_clip,
        block_valid,
        clip_frame,
        unit_tokens,
        wkv,
        latent_query_rows,
        latents,
        logit_scale.reshape(1, 1),
        wo,
        wp,
        movie_frame_embeddings,
    )
    return pl.pallas_call(
        output_kernel,
        name="outputs",
        out_shape=[jax.ShapeDtypeStruct(state.shape, BF16), jax.ShapeDtypeStruct((2,), F32)],
        in_specs=[VMEM_SPEC, VMEM_SPEC],
        out_specs=[VMEM_SPEC, SMEM_SPEC],
    )(state, loss)


def solution(mesh):
    return jax.shard_map(
        per_device,
        mesh=mesh,
        in_specs=(
            P(("sess", "dp", "fsdp"), None, None),
            P(("sess", "dp", "fsdp"), None),
            P(("sess", "dp", "fsdp")),
            P(("sess", "dp", "fsdp")),
            P(),
            P(),
            P("fsdp", None),
            P("fsdp", None),
            P("fsdp", None),
            P(),
            P(("sess", "dp", "fsdp")),
            P(),
        ),
        out_specs=(P(("sess", "dp", "fsdp"), None, None), P(("sess", "dp", "fsdp"))),
        check_vma=False,
    )
```
